32 devices in a mesh: gx: 4 (over x, core), gy: 8 (over z, y).
Axes of the slice: x: 2, y: 2, z: 4, core: 2. Of those that a mesh axis runs over, the one named last changes fastest.
Arguments:
- green_ops: bfloat16 [4, 8, 2, 1024, 1024], P('gx', 'gy'), may hold values from -0.125 to 0.125
- cell_map: int32 [4, 8, 1024], P('gx', 'gy'), may hold values from 0 to 2
- dipole_site: int32 [4, 8, 128], P('gx', 'gy'), may hold values from 0 to 1023
- dipole_amp: float32 [4, 8, 2, 128], P('gx', 'gy'), may hold values from -32 to 32
- contrast: float32 [3, 2], replicated, may hold values from 0.3 to 1
Outputs:
- traces: bfloat16 [4, 8, 1024, 2, 128], P('gx', 'gy')
The draws below stay inside these ranges and needn't reach their ends.
All inputs are finite; a program needn't handle non-finite values.
Results may differ from the reference program's by a relative error of at most 0.0069.
Values may be sent and summed in bfloat16 or wider, within the bound.
A program may use at most 64 MiB of HBM per device.

```python
import jax
import jax.numpy as jnp
from jax import lax

FACE = 512
NB = 64
MB = 2
STEPS = 4
CLASSES = 3
SUBX = 4
SUBY = 8


def plant(values, own_key, smallest, largest):
    index_at = [jax.random.randint(jax.random.fold_in(own_key, axis), (), 0, length) for axis, length in enumerate(values.shape)]
    main_axis = values.shape.index(max(values.shape))
    beside = index_at[:main_axis] + [(index_at[main_axis] + 1) % values.shape[main_axis]] + index_at[main_axis + 1:]
    return values.at[tuple(index_at)].set(smallest).at[tuple(beside)].set(largest)


def levels(stream_key, dims, split, least, high):
    factor_of = 1.0
    for position, shards_of in split:
        steps = jax.random.uniform(jax.random.fold_in(jax.random.fold_in(stream_key, 6), position), (shards_of,), jnp.float32, least / len(split), high / len(split))
        factor_of = factor_of * jnp.repeat(jnp.exp(steps), dims[position] // shards_of).reshape((-1,) + (1,) * (len(dims) - 1 - position))
    return factor_of


def gaussian(stream_key, extent, deviation, reach, cuts=(), dtype=jnp.bfloat16):
    gain = levels(stream_key, extent, cuts, -0.22, 0.18) if cuts else 1.0
    entries = jax.random.normal(stream_key, extent, jnp.float32) * deviation * gain
    return jnp.minimum(jnp.maximum(entries, -reach), reach).astype(dtype)


def setup_inputs(seed: int = 0) -> dict:
    arg_keys = jax.random.split(jax.random.key(seed), 6)
    green_ops = gaussian(arg_keys[0], (SUBX, SUBY, 2, 2 * FACE, 2 * FACE), (4 * FACE) ** -0.5, 0.125, ((0, 4), (1, 8)))
    cell_map = plant(jax.random.randint(arg_keys[1], (SUBX, SUBY, 2 * FACE), 0, CLASSES), jax.random.fold_in(arg_keys[1], 1), 0, CLASSES - 1).astype(jnp.int32)
    dipole_site = plant(jax.random.randint(arg_keys[2], (SUBX, SUBY, MB * NB), 0, 2 * FACE), jax.random.fold_in(arg_keys[2], 1), 0, (2 * FACE) - 1).astype(jnp.int32)
    dipole_amp = jnp.clip(jax.random.uniform(arg_keys[3], (SUBX, SUBY, 2, MB * NB), jnp.float32, -32.0, 32.0) * levels(arg_keys[3], (SUBX, SUBY, 2, MB * NB), ((0, 4), (1, 8)), -0.4, 0.0), -32.0, 32.0)
    contrast = jnp.clip(jax.random.uniform(arg_keys[4], (CLASSES, 2), jnp.float32, 0.3, 1.0), 0.3, 1.0)
    return {"green_ops": green_ops, "cell_map": cell_map, "dipole_site": dipole_site, "dipole_amp": dipole_amp, "contrast": contrast}


def apply_row(pair):
    ops_row, excited_row = pair
    ops_wide = ops_row.astype(jnp.float32)
    data_wide = excited_row.astype(jnp.float32)
    product = jnp.einsum('jspq,jqrc->jsprc', ops_wide, data_wide, precision=lax.Precision.HIGHEST)
    real_out = product[:, 0, :, 0] - product[:, 1, :, 1]
    imag_out = product[:, 0, :, 1] + product[:, 1, :, 0]
    return jnp.stack([real_out, imag_out], axis=2).astype(jnp.bfloat16)


def reference(green_ops, cell_map, dipole_site, dipole_amp, contrast):
    trace_rows = 2 * FACE
    columns = MB * NB
    one_hot = (lax.broadcasted_iota(jnp.int32, (SUBX, SUBY, trace_rows, columns), 2) == dipole_site[:, :, None, :]).astype(jnp.float32)
    source = one_hot[:, :, :, None, :] * dipole_amp[:, :, None, :, :]
    factor = contrast[cell_map]
    real_factor = factor[..., 0][..., None]
    imag_factor = factor[..., 1][..., None]
    batch_index = lax.broadcasted_iota(jnp.int32, (columns,), 0) // NB
    traces = jnp.zeros((SUBX, SUBY, trace_rows, 2, columns), jnp.bfloat16)
    for turn_index in range(STEPS):
        east_trace = traces[:, :, :FACE]
        north_trace = traces[:, :, FACE:]
        west_trace = jnp.concatenate([jnp.zeros_like(east_trace[:1]), east_trace[:-1]], axis=0)
        south_trace = jnp.concatenate([jnp.zeros_like(north_trace[:, :1]), north_trace[:, :-1]], axis=1)
        incoming = jnp.concatenate([west_trace, south_trace], axis=2).astype(jnp.float32)
        real_in = real_factor * incoming[..., 0, :] - imag_factor * incoming[..., 1, :] + source[..., 0, :]
        imag_in = real_factor * incoming[..., 1, :] + imag_factor * incoming[..., 0, :] + source[..., 1, :]
        excited = jnp.stack([real_in, imag_in], axis=3).astype(jnp.bfloat16)
        image = lax.map(apply_row, (green_ops, excited))
        traces = jnp.where(batch_index <= turn_index, image, jnp.zeros_like(image))
    return traces
```

```python
import functools

import jax
import jax.numpy as jnp
from jax import lax
from jax.experimental import pallas as pl
from jax.experimental.pallas import tpu as pltpu
from jax.sharding import PartitionSpec as P

MB = 2
STEPS = 4
CHUNKS = 2
TURNS = MB * STEPS - 1
SENDS = TURNS - MB
MESH = pl.DeviceIdType.MESH


def kernel(
    nx, ny, ops_hbm, cells_hbm, site_hbm, amp_hbm, contrast_hbm, out_ref,
    ops, cells, site, amp, contrast, site_of, amp_of, fac, excited, west, south, east_out, north_out, last_b, wide,
    ops_sem, small_sem, send_sem, recv_sem,
):
    i = lax.axis_index("gx")
    j = lax.axis_index("gy")
    rows = ops.shape[1]
    face = rows // 2
    lanes = site.shape[1]
    nb = lanes // 2
    piece = face // CHUNKS

    def ops_copy(k):
        block = pl.ds(face if k == 0 else 0, face)
        return pltpu.make_async_copy(ops_hbm.at[:, block], ops.at[:, block], ops_sem.at[k])

    small = [
        pltpu.make_async_copy(src, dst, small_sem.at[k])
        for k, (src, dst) in enumerate(
            [(site_hbm, site), (amp_hbm, amp), (cells_hbm, cells), (contrast_hbm, contrast)]
        )
    ]
    for copy in small:
        copy.start()
    ops_copy(0).start()
    ops_copy(1).start()

    barrier = pltpu.get_barrier_semaphore()

    @pl.when(i > 0)
    def _():
        pl.semaphore_signal(barrier, inc=1, device_id={"gx": i - 1}, device_id_type=MESH)

    @pl.when(j > 0)
    def _():
        pl.semaphore_signal(barrier, inc=1, device_id={"gy": j - 1}, device_id_type=MESH)

    for copy in small:
        copy.wait()

    low = lax.broadcasted_iota(jnp.int32, (1, lanes), 1) < nb
    sites = site[...]
    sites_turned = pltpu.roll(sites, nb, axis=1)
    site_of[0] = jnp.where(low, sites, sites_turned)
    site_of[1] = jnp.where(low, sites_turned, sites)
    real, imag = amp[0:1, :], amp[1:2, :]
    real_turned, imag_turned = pltpu.roll(real, nb, axis=1), pltpu.roll(imag, nb, axis=1)
    amp_of[0, 0] = jnp.where(low, real, imag_turned)
    amp_of[1, 0] = jnp.where(low, real_turned, imag)
    amp_of[0, 1] = jnp.where(low, -imag, real_turned)
    amp_of[1, 1] = jnp.where(low, -imag_turned, real)

    classes = contrast.shape[1]
    for a in range(rows // lanes):
        column = jnp.broadcast_to(cells[a : a + 1, :], (lanes, lanes)).T
        for c in range(2):
            value = jnp.full((lanes, lanes), contrast[c, 0], jnp.float32)
            for k in range(1, classes):
                value = jnp.where(column == k, contrast[c, k], value)
            fac[c, pl.ds(a * lanes, lanes), :] = value

    @pl.when(i == 0)
    def _():
        west[...] = jnp.zeros_like(west)

    @pl.when(j == 0)
    def _():
        south[...] = jnp.zeros_like(south)

    targets = jnp.where(i < nx - 1, 1, 0) + jnp.where(j < ny - 1, 1, 0)

    @pl.when(targets > 0)
    def _():
        pl.semaphore_wait(barrier, targets)

    def send(direction, turn, part):
        block = pl.ds(part * piece, piece)
        source, target, to = (
            (north_out, south, {"gy": j + 1}) if direction == 0 else (east_out, west, {"gx": i + 1})
        )
        return pltpu.make_async_remote_copy(
            src_ref=source.at[turn, block],
            dst_ref=target.at[turn, block],
            send_sem=send_sem.at[direction, turn, part],
            recv_sem=recv_sem.at[direction, turn, part],
            device_id=to,
            device_id_type=MESH,
        )

    has_target = (j < ny - 1, i < nx - 1)
    has_source = (j > 0, i > 0)

    def source_term(m, offset, size):
        points = lax.broadcasted_iota(jnp.int32, (size, lanes), 0) + offset
        hit = points == site_of[m]
        return (
            jnp.where(hit, amp_of[m, 0], 0.0),
            jnp.where(hit, amp_of[m, 1], 0.0),
        )

    def turn_body(turn, _):
        m = turn % MB

        @pl.when(turn < MB)
        def _():
            for a in range(rows // piece):
                block = pl.ds(a * piece, piece)
                y, iy = source_term(m, a * piece, piece)
                excited[0, block, :] = y.astype(jnp.bfloat16)
                excited[1, block, :] = iy.astype(jnp.bfloat16)

        @pl.when(turn >= MB)
        def _():
            for direction, buffer, base in ((1, west, 0), (0, south, face)):
                for part in range(CHUNKS):
                    @pl.when(has_source[direction])
                    def _():
                        send(direction, turn - MB, part).wait_recv()

                    offset = base + part * piece
                    x = buffer[turn - MB, pl.ds(part * piece, piece), :].astype(jnp.float32)
                    turned = pltpu.roll(x, nb, axis=1)
                    ix = jnp.where(low, -turned, turned)
                    y0, iy0 = source_term(m, offset, piece)
                    block = pl.ds(offset, piece)
                    fr, fi = fac[0, block, :], fac[1, block, :]
                    excited[0, block, :] = (fr * x + fi * ix + y0).astype(jnp.bfloat16)
                    excited[1, block, :] = (fr * ix - fi * x + iy0).astype(jnp.bfloat16)

        for direction, base in ((0, face), (1, 0)):
            @pl.when(turn == 0)
            def _():
                ops_copy(direction).wait()

            for part in range(CHUNKS):
                block = pl.ds(base + part * piece, piece)
                image = jnp.dot(
                    ops[0, block, :], excited[0], preferred_element_type=jnp.float32
                ) + jnp.dot(ops[1, block, :], excited[1], preferred_element_type=jnp.float32)

                @pl.when(turn < SENDS)
                def _():
                    held = north_out if direction == 0 else east_out
                    held[turn, pl.ds(part * piece, piece), :] = image.astype(jnp.bfloat16)

                    @pl.when(has_target[direction])
                    def _():
                        send(direction, turn, part).start()

                @pl.when(turn == TURNS - 2)
                def _():
                    last_b[block, :] = image

                @pl.when(turn == TURNS - 1)
                def _():
                    other = last_b[block, :]
                    start = 2 * (base + part * piece)
                    wide[pl.ds(start, piece, stride=2), :] = jnp.where(
                        low, image, pltpu.roll(other, nb, axis=1)
                    )
                    wide[pl.ds(start + 1, piece, stride=2), :] = jnp.where(
                        low, pltpu.roll(image, nb, axis=1), other
                    )
                    both = pl.ds(start, 2 * piece)
                    out_ref[both, :] = wide[both, :].astype(jnp.bfloat16)

        return 0

    lax.fori_loop(0, TURNS, turn_body, 0)

    for direction in (0, 1):
        @pl.when(has_target[direction])
        def _():
            for turn in range(SENDS):
                for part in range(CHUNKS):
                    send(direction, turn, part).wait_send()


def per_device(nx, ny, green_ops, cell_map, dipole_site, dipole_amp, contrast):
    rows = green_ops.shape[-1]
    lanes = dipole_site.shape[-1]
    face = rows // 2
    bf16, f32, i32 = jnp.bfloat16, jnp.float32, jnp.int32
    out = pl.pallas_call(
        functools.partial(kernel, nx, ny),
        out_shape=jax.ShapeDtypeStruct((2 * rows, lanes), bf16),
        in_specs=[pl.BlockSpec(memory_space=pl.ANY)] * 5,
        out_specs=pl.BlockSpec(memory_space=pltpu.VMEM),
        scratch_shapes=[
            pltpu.VMEM((2, rows, rows), bf16),
            pltpu.VMEM((rows // lanes, lanes), i32),
            pltpu.VMEM((1, lanes), i32),
            pltpu.VMEM((2, lanes), f32),
            pltpu.SMEM(contrast.shape[::-1], f32),
            pltpu.VMEM((MB, 1, lanes), i32),
            pltpu.VMEM((MB, 2, 1, lanes), f32),
            pltpu.VMEM((2, rows, lanes), f32),
            pltpu.VMEM((2, rows, lanes), bf16),
            pltpu.VMEM((SENDS, face, lanes), bf16),
            pltpu.VMEM((SENDS, face, lanes), bf16),
            pltpu.VMEM((SENDS, face, lanes), bf16),
            pltpu.VMEM((SENDS, face, lanes), bf16),
            pltpu.VMEM((rows, lanes), f32),
            pltpu.VMEM((2 * rows, lanes), f32),
            pltpu.SemaphoreType.DMA((2,)),
            pltpu.SemaphoreType.DMA((4,)),
            pltpu.SemaphoreType.DMA((2, SENDS, CHUNKS)),
            pltpu.SemaphoreType.DMA((2, SENDS, CHUNKS)),
        ],
        compiler_params=pltpu.CompilerParams(collective_id=0, has_side_effects=True),
    )(
        green_ops[0, 0],
        cell_map.reshape(rows // lanes, lanes),
        dipole_site.reshape(1, lanes),
        dipole_amp[0, 0],
        contrast.T,
    )
    return out.reshape(1, 1, rows, 2, lanes)


def solution(mesh):
    placed = (
        P("gx", "gy", None, None, None),
        P("gx", "gy", None),
        P("gx", "gy", None),
        P("gx", "gy", None, None),
        P(),
    )
    return jax.shard_map(
        functools.partial(per_device, mesh.shape["gx"], mesh.shape["gy"]),
        mesh=mesh,
        in_specs=placed,
        out_specs=P("gx", "gy", None, None, None),
        check_vma=False,
    )
```

```python
import functools

import jax
import jax.numpy as jnp
from jax import lax
from jax.experimental import pallas as pl
from jax.experimental.pallas import tpu as pltpu
from jax.sharding import PartitionSpec as P

MB = 2
STEPS = 4
CHUNKS = 2
TURNS = MB * STEPS - 1
SENDS = TURNS - MB
MESH = pl.DeviceIdType.MESH


def kernel(
    nx, ny, ops_hbm, cells_hbm, site_hbm, amp_hbm, contrast_hbm, out_ref,
    ops, cells, site, amp, contrast, site_of, amp_of, fac, excited, west, south, east_out, north_out, last_b, wide,
    ops_sem, small_sem, send_sem, recv_sem,
):
    i = lax.axis_index("gx")
    j = lax.axis_index("gy")
    rows = ops.shape[1]
    face = rows // 2
    lanes = site.shape[1]
    nb = lanes // 2
    piece = face // CHUNKS

    def ops_copy(k):
        block = pl.ds(face if k == 0 else 0, face)
        return pltpu.make_async_copy(ops_hbm.at[:, block], ops.at[:, block], ops_sem.at[k])

    small = [
        pltpu.make_async_copy(src, dst, small_sem.at[k])
        for k, (src, dst) in enumerate(
            [(site_hbm, site), (amp_hbm, amp), (cells_hbm, cells), (contrast_hbm, contrast)]
        )
    ]
    for copy in small:
        copy.start()
    ops_copy(0).start()
    ops_copy(1).start()

    barrier = pltpu.get_barrier_semaphore()

    @pl.when(i > 0)
    def _():
        pl.semaphore_signal(barrier, inc=1, device_id={"gx": i - 1}, device_id_type=MESH)

    @pl.when(j > 0)
    def _():
        pl.semaphore_signal(barrier, inc=1, device_id={"gy": j - 1}, device_id_type=MESH)

    for copy in small:
        copy.wait()

    low = lax.broadcasted_iota(jnp.int32, (1, lanes), 1) < nb
    sites = site[...]
    sites_turned = pltpu.roll(sites, nb, axis=1)
    site_of[0] = jnp.where(low, sites, sites_turned)
    site_of[1] = jnp.where(low, sites_turned, sites)
    real, imag = amp[0:1, :], amp[1:2, :]
    real_turned, imag_turned = pltpu.roll(real, nb, axis=1), pltpu.roll(imag, nb, axis=1)
    amp_of[0, 0] = jnp.where(low, real, imag_turned)
    amp_of[1, 0] = jnp.where(low, real_turned, imag)
    amp_of[0, 1] = jnp.where(low, -imag, real_turned)
    amp_of[1, 1] = jnp.where(low, -imag_turned, real)

    classes = contrast.shape[1]
    for a in range(rows // lanes):
        column = jnp.broadcast_to(cells[a : a + 1, :], (lanes, lanes)).T
        for c in range(2):
            value = jnp.full((lanes, lanes), contrast[c, 0], jnp.float32)
            for k in range(1, classes):
                value = jnp.where(column == k, contrast[c, k], value)
            fac[c, pl.ds(a * lanes, lanes), :] = value

    @pl.when(i == 0)
    def _():
        west[...] = jnp.zeros_like(west)

    @pl.when(j == 0)
    def _():
        south[...] = jnp.zeros_like(south)

    targets = jnp.where(i < nx - 1, 1, 0) + jnp.where(j < ny - 1, 1, 0)

    @pl.when(targets > 0)
    def _():
        pl.semaphore_wait(barrier, targets)

    def send(direction, turn, part):
        block = pl.ds(part * piece, piece)
        source, target, to = (
            (north_out, south, {"gy": j + 1}) if direction == 0 else (east_out, west, {"gx": i + 1})
        )
        return pltpu.make_async_remote_copy(
            src_ref=source.at[turn, block],
            dst_ref=target.at[turn, block],
            send_sem=send_sem.at[direction, turn, part],
            recv_sem=recv_sem.at[direction, turn, part],
            device_id=to,
            device_id_type=MESH,
        )

    has_target = (j < ny - 1, i < nx - 1)
    has_source = (j > 0, i > 0)

    def source_term(m, offset, size):
        points = lax.broadcasted_iota(jnp.int32, (size, lanes), 0) + offset
        hit = points == site_of[m]
        return (
            jnp.where(hit, amp_of[m, 0], 0.0),
            jnp.where(hit, amp_of[m, 1], 0.0),
        )

    def turn_body(turn, _):
        m = turn % MB

        @pl.when(turn < MB)
        def _():
            for a in range(rows // piece):
                block = pl.ds(a * piece, piece)
                y, iy = source_term(m, a * piece, piece)
                excited[0, block, :] = y.astype(jnp.bfloat16)
                excited[1, block, :] = iy.astype(jnp.bfloat16)

        @pl.when(turn >= MB)
        def _():
            for direction, buffer, base in ((1, west, 0), (0, south, face)):
                for part in range(CHUNKS):
                    @pl.when(has_source[direction])
                    def _():
                        send(direction, turn - MB, part).wait_recv()

                    offset = base + part * piece
                    x = buffer[turn - MB, pl.ds(part * piece, piece), :].astype(jnp.float32)
                    turned = pltpu.roll(x, nb, axis=1)
                    ix = jnp.where(low, -turned, turned)
                    y0, iy0 = source_term(m, offset, piece)
                    block = pl.ds(offset, piece)
                    fr, fi = fac[0, block, :], fac[1, block, :]
                    excited[0, block, :] = (fr * x + fi * ix + y0).astype(jnp.bfloat16)
                    excited[1, block, :] = (fr * ix - fi * x + iy0).astype(jnp.bfloat16)

        for direction, base in ((0, face), (1, 0)):
            @pl.when(turn == 0)
            def _():
                ops_copy(direction).wait()

            for part in range(CHUNKS):
                block = pl.ds(base + part * piece, piece)
                image = jnp.dot(
                    ops[0, block, :], excited[0], preferred_element_type=jnp.float32
                ) + jnp.dot(ops[1, block, :], excited[1], preferred_element_type=jnp.float32)

                @pl.when(turn < SENDS)
                def _():
                    held = north_out if direction == 0 else east_out
                    held[turn, pl.ds(part * piece, piece), :] = image.astype(jnp.bfloat16)

                    @pl.when(has_target[direction])
                    def _():
                        send(direction, turn, part).start()

                @pl.when(turn == TURNS - 2)
                def _():
                    last_b[block, :] = image

                @pl.when(turn == TURNS - 1)
                def _():
                    other = last_b[block, :]
                    start = 2 * (base + part * piece)
                    wide[pl.ds(start, piece, stride=2), :] = jnp.where(
                        low, image, pltpu.roll(other, nb, axis=1)
                    )
                    wide[pl.ds(start + 1, piece, stride=2), :] = jnp.where(
                        low, pltpu.roll(image, nb, axis=1), other
                    )
                    both = pl.ds(start, 2 * piece)
                    out_ref[both, :] = wide[both, :].astype(jnp.bfloat16)

        return 0

    lax.fori_loop(0, TURNS, turn_body, 0)

    for direction in (0, 1):
        @pl.when(has_target[direction])
        def _():
            for turn in range(SENDS):
                for part in range(CHUNKS):
                    send(direction, turn, part).wait_send()


def per_device(nx, ny, green_ops, cell_map, dipole_site, dipole_amp, contrast):
    rows = green_ops.shape[-1]
    lanes = dipole_site.shape[-1]
    face = rows // 2
    bf16, f32, i32 = jnp.bfloat16, jnp.float32, jnp.int32
    out = pl.pallas_call(
        functools.partial(kernel, nx, ny),
        out_shape=pltpu.VMEM((2 * rows, lanes), bf16),
        in_specs=[pl.BlockSpec(memory_space=pl.ANY)] * 5,
        out_specs=pl.BlockSpec(memory_space=pltpu.VMEM),
        scratch_shapes=[
            pltpu.VMEM((2, rows, rows), bf16),
            pltpu.VMEM((rows // lanes, lanes), i32),
            pltpu.VMEM((1, lanes), i32),
            pltpu.VMEM((2, lanes), f32),
            pltpu.SMEM(contrast.shape[::-1], f32),
            pltpu.VMEM((MB, 1, lanes), i32),
            pltpu.VMEM((MB, 2, 1, lanes), f32),
            pltpu.VMEM((2, rows, lanes), f32),
            pltpu.VMEM((2, rows, lanes), bf16),
            pltpu.VMEM((SENDS, face, lanes), bf16),
            pltpu.VMEM((SENDS, face, lanes), bf16),
            pltpu.VMEM((SENDS, face, lanes), bf16),
            pltpu.VMEM((SENDS, face, lanes), bf16),
            pltpu.VMEM((rows, lanes), f32),
            pltpu.VMEM((2 * rows, lanes), f32),
            pltpu.SemaphoreType.DMA((2,)),
            pltpu.SemaphoreType.DMA((4,)),
            pltpu.SemaphoreType.DMA((2, SENDS, CHUNKS)),
            pltpu.SemaphoreType.DMA((2, SENDS, CHUNKS)),
        ],
        compiler_params=pltpu.CompilerParams(collective_id=0, has_side_effects=True),
    )(
        green_ops[0, 0],
        cell_map.reshape(rows // lanes, lanes),
        dipole_site.reshape(1, lanes),
        dipole_amp[0, 0],
        contrast.T,
    )
    return out.reshape(1, 1, rows, 2, lanes)


def solution(mesh):
    placed = (
        P("gx", "gy", None, None, None),
        P("gx", "gy", None),
        P("gx", "gy", None),
        P("gx", "gy", None, None),
        P(),
    )
    return jax.shard_map(
        functools.partial(per_device, mesh.shape["gx"], mesh.shape["gy"]),
        mesh=mesh,
        in_specs=placed,
        out_specs=P("gx", "gy", None, None, None),
        check_vma=False,
    )
```

```python
import functools

import jax
import jax.numpy as jnp
from jax import lax
from jax.experimental import pallas as pl
from jax.experimental.pallas import tpu as pltpu
from jax.sharding import PartitionSpec as P

MB = 2
STEPS = 4
CHUNKS = 2
TURNS = MB * STEPS - 1
SENDS = TURNS - MB
MESH = pl.DeviceIdType.MESH


def kernel(
    nx, ny, ops_hbm, cells_hbm, site_hbm, amp_hbm, contrast_hbm, out_ref,
    ops, ops_t, cells, site, amp, contrast, site_col, amp_col, fac, first, excited, total,
    west, south, east_out, north_out, final, wide, ops_sem, small_sem, send_sem, recv_sem,
):
    i = lax.axis_index("gx")
    j = lax.axis_index("gy")
    rows = ops.shape[1]
    face = rows // 2
    lanes = site.shape[1]
    nb = lanes // 2
    piece = face // CHUNKS
    bf16, f32 = jnp.bfloat16, jnp.float32
    bases = (face, 0)

    def ops_copy(direction, part):
        block = pl.ds(bases[direction] + part * piece, piece)
        return pltpu.make_async_copy(
            ops_hbm.at[:, block], ops.at[:, block], ops_sem.at[direction, part]
        )

    small = [
        pltpu.make_async_copy(src, dst, small_sem.at[k])
        for k, (src, dst) in enumerate(
            [(site_hbm, site), (amp_hbm, amp), (cells_hbm, cells), (contrast_hbm, contrast)]
        )
    ]
    for copy in small:
        copy.start()
    for direction in range(2):
        for part in range(CHUNKS):
            ops_copy(direction, part).start()

    barrier = pltpu.get_barrier_semaphore()

    @pl.when(i > 0)
    def _():
        pl.semaphore_signal(barrier, inc=1, device_id={"gx": i - 1}, device_id_type=MESH)

    @pl.when(j > 0)
    def _():
        pl.semaphore_signal(barrier, inc=1, device_id={"gy": j - 1}, device_id_type=MESH)

    for copy in small:
        copy.wait()

    low = lax.broadcasted_iota(jnp.int32, (1, lanes), 1) < nb
    sites = site[...]
    sites_turned = pltpu.roll(sites, nb, axis=1)
    real, imag = amp[0:1, :], amp[1:2, :]
    real_turned, imag_turned = pltpu.roll(real, nb, axis=1), pltpu.roll(imag, nb, axis=1)
    site_row = (jnp.where(low, sites, sites_turned), jnp.where(low, sites_turned, sites))
    amp_row = (jnp.where(low, real, imag_turned), jnp.where(low, real_turned, imag))
    turned_row = (jnp.where(low, -imag, real_turned), jnp.where(low, -imag_turned, real))
    for a in range(rows // lanes):
        block = pl.ds(a * lanes, lanes)
        points = lax.broadcasted_iota(jnp.int32, (lanes, lanes), 0) + a * lanes
        for m in range(MB):
            hit = points == site_row[m]
            columns = pl.ds(m * lanes, lanes)
            first[0, block, columns] = jnp.where(hit, amp_row[m], 0.0).astype(bf16)
            first[1, block, columns] = jnp.where(hit, turned_row[m], 0.0).astype(bf16)

    targets = jnp.where(i < nx - 1, 1, 0) + jnp.where(j < ny - 1, 1, 0)

    @pl.when(targets > 0)
    def _():
        pl.semaphore_wait(barrier, targets)

    def send(direction, turn, part):
        source, target, to = (
            (north_out, south, {"gy": j + 1}) if direction == 0 else (east_out, west, {"gx": i + 1})
        )
        return pltpu.make_async_remote_copy(
            src_ref=source.at[turn, part],
            dst_ref=target.at[turn, part],
            send_sem=send_sem.at[direction, turn, part],
            recv_sem=recv_sem.at[direction, turn, part],
            device_id=to,
            device_id_type=MESH,
        )

    has_target = (j < ny - 1, i < nx - 1)
    has_source = (j > 0, i > 0)

    for direction in range(2):
        held = (north_out, east_out)[direction]
        for part in range(CHUNKS):
            ops_copy(direction, part).wait()
            block = pl.ds(bases[direction] + part * piece, piece)
            image = jnp.dot(ops[0, block, :], first[0], preferred_element_type=f32) + jnp.dot(
                ops[1, block, :], first[1], preferred_element_type=f32
            )
            for m in range(MB):
                held[m, part] = image[:, m * lanes : (m + 1) * lanes].T.astype(bf16)

            @pl.when(has_target[direction])
            def _():
                send(direction, 0, part).start()

        @pl.when(has_target[direction])
        def _():
            for part in range(CHUNKS):
                send(direction, 1, part).start()

    @pl.when(i == 0)
    def _():
        west[...] = jnp.zeros_like(west)

    @pl.when(j == 0)
    def _():
        south[...] = jnp.zeros_like(south)

    for m in range(MB):
        site_col[m] = jnp.broadcast_to(site_row[m], (lanes, lanes)).T
        amp_col[m] = jnp.broadcast_to(amp_row[m], (lanes, lanes)).T
    for c in range(2):
        value = jnp.full(cells.shape, contrast[c, 0], f32)
        for k in range(1, contrast.shape[1]):
            value = jnp.where(cells[...] == k, contrast[c, k], value)
        fac[c] = value
    for c in range(2):
        for a in range(rows // lanes):
            block = pl.ds(a * lanes, lanes)
            ops_t[c, :, block] = ops[c, block, :].T

    def excite(m, buffer, slot, base):
        for a in range(face // lanes):
            part, inner = divmod(a * lanes, piece)
            x = buffer[slot, part, :, pl.ds(inner, lanes)].astype(f32)
            row = base // lanes + a
            fr, fi = fac[0, pl.ds(row, 1), :], fac[1, pl.ds(row, 1), :]
            points = lax.broadcasted_iota(jnp.int32, (lanes, lanes), 1) + row * lanes
            source = jnp.where(points == site_col[m], amp_col[m], 0.0)
            y_real = (fr * x[:nb] - fi * x[nb:] + source[:nb]).astype(bf16)
            y_imag = (fr * x[nb:] + fi * x[:nb] + source[nb:]).astype(bf16)
            block = pl.ds(base + a * lanes, lanes)
            excited[0, :nb, block] = y_real
            excited[0, nb:, block] = y_imag
            excited[1, :nb, block] = -y_imag
            excited[1, nb:, block] = y_real

    def product(depth, columns):
        return jnp.dot(
            excited[0, :, depth], ops_t[0, depth, columns], preferred_element_type=f32
        ) + jnp.dot(excited[1, :, depth], ops_t[1, depth, columns], preferred_element_type=f32)

    def turn_body(turn, _):
        m = turn % MB
        slot = turn - MB

        @pl.when(has_source[1])
        def _():
            for part in range(CHUNKS):
                send(1, slot, part).wait_recv()

        excite(m, west, slot, 0)
        total[...] = product(slice(0, face), slice(0, rows))

        @pl.when(has_source[0])
        def _():
            for part in range(CHUNKS):
                send(0, slot, part).wait_recv()

        excite(m, south, slot, face)
        for direction in range(2):
            held = (north_out, east_out)[direction]
            for part in range(CHUNKS):
                start = bases[direction] + part * piece
                columns = slice(start, start + piece)
                image = total[:, columns] + product(slice(face, rows), columns)

                @pl.when(turn < SENDS)
                def _():
                    held[turn, part] = image.astype(bf16)

                    @pl.when(has_target[direction])
                    def _():
                        send(direction, turn, part).start()

                @pl.when(turn == TURNS - 2)
                def _():
                    final[0, nb:, columns] = image[:nb]
                    final[1, nb:, columns] = image[nb:]

                @pl.when(turn == TURNS - 1)
                def _():
                    final[0, :nb, columns] = image[:nb]
                    final[1, :nb, columns] = image[nb:]
                    for a in range(start, start + piece, lanes):
                        for c in range(2):
                            wide[pl.ds(2 * a + c, lanes, stride=2), :] = final[c, :, a : a + lanes].T
                        both = pl.ds(2 * a, 2 * lanes)
                        out_ref[both, :] = wide[both, :].astype(bf16)

        return 0

    lax.fori_loop(MB, TURNS, turn_body, 0)

    for direction in (0, 1):
        @pl.when(has_target[direction])
        def _():
            for turn in range(SENDS):
                for part in range(CHUNKS):
                    send(direction, turn, part).wait_send()


def per_device(nx, ny, green_ops, cell_map, dipole_site, dipole_amp, contrast):
    rows = green_ops.shape[-1]
    lanes = dipole_site.shape[-1]
    face = rows // 2
    bf16, f32, i32 = jnp.bfloat16, jnp.float32, jnp.int32
    out = pl.pallas_call(
        functools.partial(kernel, nx, ny),
        out_shape=pltpu.VMEM((2 * rows, lanes), bf16),
        in_specs=[pl.BlockSpec(memory_space=pl.ANY)] * 5,
        out_specs=pl.BlockSpec(memory_space=pltpu.VMEM),
        scratch_shapes=[
            pltpu.VMEM((2, rows, rows), bf16),
            pltpu.VMEM((2, rows, rows), bf16),
            pltpu.VMEM((rows // lanes, lanes), i32),
            pltpu.VMEM((1, lanes), i32),
            pltpu.VMEM((2, lanes), f32),
            pltpu.SMEM(contrast.shape[::-1], f32),
            pltpu.VMEM((MB, lanes, lanes), i32),
            pltpu.VMEM((MB, lanes, lanes), f32),
            pltpu.VMEM((2, rows // lanes, lanes), f32),
            pltpu.VMEM((2, rows, MB * lanes), bf16),
            pltpu.VMEM((2, lanes, rows), bf16),
            pltpu.VMEM((lanes, rows), f32),
            *[pltpu.VMEM((SENDS, CHUNKS, lanes, face // CHUNKS), bf16)] * 4,
            pltpu.VMEM((2, lanes, rows), f32),
            pltpu.VMEM((2 * rows, lanes), f32),
            pltpu.SemaphoreType.DMA((2, CHUNKS)),
            pltpu.SemaphoreType.DMA((4,)),
            pltpu.SemaphoreType.DMA((2, SENDS, CHUNKS)),
            pltpu.SemaphoreType.DMA((2, SENDS, CHUNKS)),
        ],
        compiler_params=pltpu.CompilerParams(collective_id=0, has_side_effects=True),
    )(
        green_ops[0, 0],
        cell_map.reshape(rows // lanes, lanes),
        dipole_site.reshape(1, lanes),
        dipole_amp[0, 0],
        contrast.T,
    )
    return out.reshape(1, 1, rows, 2, lanes)


def solution(mesh):
    placed = (
        P("gx", "gy", None, None, None),
        P("gx", "gy", None),
        P("gx", "gy", None),
        P("gx", "gy", None, None),
        P(),
    )
    return jax.shard_map(
        functools.partial(per_device, mesh.shape["gx"], mesh.shape["gy"]),
        mesh=mesh,
        in_specs=placed,
        out_specs=P("gx", "gy", None, None, None),
        check_vma=False,
    )
```

```python
import functools

import jax
import jax.numpy as jnp
from jax import lax
from jax.experimental import pallas as pl
from jax.experimental.pallas import tpu as pltpu
from jax.sharding import PartitionSpec as P

MB = 2
STEPS = 4
CHUNKS = 2
TURNS = MB * STEPS - 1
SENDS = TURNS - MB
MESH = pl.DeviceIdType.MESH


def kernel(
    nx, ny, ops_hbm, cells_hbm, site_hbm, amp_hbm, contrast_hbm, out_ref,
    ops, ops_t, cells, site, amp, contrast, site_col, amp_col, fac, first, excited, total,
    west, south, east_out, north_out, final, order, ops_sem, small_sem, send_sem, recv_sem,
):
    i = lax.axis_index("gx")
    j = lax.axis_index("gy")
    rows = ops.shape[1]
    face = rows // 2
    lanes = site.shape[1]
    nb = lanes // 2
    piece = face // CHUNKS
    bf16, f32 = jnp.bfloat16, jnp.float32
    bases = (face, 0)

    def ops_copy(direction, part):
        block = pl.ds(bases[direction] + part * piece, piece)
        return pltpu.make_async_copy(
            ops_hbm.at[:, block], ops.at[:, block], ops_sem.at[direction, part]
        )

    small = [
        pltpu.make_async_copy(src, dst, small_sem.at[k])
        for k, (src, dst) in enumerate(
            [(site_hbm, site), (amp_hbm, amp), (cells_hbm, cells), (contrast_hbm, contrast)]
        )
    ]
    for copy in small:
        copy.start()
    for direction in range(2):
        for part in range(CHUNKS):
            ops_copy(direction, part).start()

    barrier = pltpu.get_barrier_semaphore()

    @pl.when(i > 0)
    def _():
        pl.semaphore_signal(barrier, inc=1, device_id={"gx": i - 1}, device_id_type=MESH)

    @pl.when(j > 0)
    def _():
        pl.semaphore_signal(barrier, inc=1, device_id={"gy": j - 1}, device_id_type=MESH)

    for copy in small[:2]:
        copy.wait()

    low = lax.broadcasted_iota(jnp.int32, (1, lanes), 1) < nb
    sites = site[...]
    sites_turned = pltpu.roll(sites, nb, axis=1)
    real, imag = amp[0:1, :], amp[1:2, :]
    real_turned, imag_turned = pltpu.roll(real, nb, axis=1), pltpu.roll(imag, nb, axis=1)
    site_row = (jnp.where(low, sites, sites_turned), jnp.where(low, sites_turned, sites))
    amp_row = (jnp.where(low, real, imag_turned), jnp.where(low, real_turned, imag))
    turned_row = (jnp.where(low, -imag, real_turned), jnp.where(low, -imag_turned, real))
    for a in range(rows // lanes):
        block = pl.ds(a * lanes, lanes)
        points = lax.broadcasted_iota(jnp.int32, (lanes, lanes), 0) + a * lanes
        for m in range(MB):
            hit = points == site_row[m]
            columns = pl.ds(m * lanes, lanes)
            first[0, block, columns] = jnp.where(hit, amp_row[m], 0.0).astype(bf16)
            first[1, block, columns] = jnp.where(hit, turned_row[m], 0.0).astype(bf16)

    targets = jnp.where(i < nx - 1, 1, 0) + jnp.where(j < ny - 1, 1, 0)

    @pl.when(targets > 0)
    def _():
        pl.semaphore_wait(barrier, targets)

    def send(direction, turn, part):
        source, target, to = (
            (north_out, south, {"gy": j + 1}) if direction == 0 else (east_out, west, {"gx": i + 1})
        )
        return pltpu.make_async_remote_copy(
            src_ref=source.at[turn, part],
            dst_ref=target.at[turn, part],
            send_sem=send_sem.at[direction, turn, part],
            recv_sem=recv_sem.at[direction, turn, part],
            device_id=to,
            device_id_type=MESH,
        )

    has_target = (j < ny - 1, i < nx - 1)
    has_source = (j > 0, i > 0)

    for direction in range(2):
        held = (north_out, east_out)[direction]
        for part in range(CHUNKS):
            ops_copy(direction, part).wait()
            block = pl.ds(bases[direction] + part * piece, piece)
            image = jnp.dot(ops[0, block, :], first[0], preferred_element_type=f32) + jnp.dot(
                ops[1, block, :], first[1], preferred_element_type=f32
            )
            image = image.astype(bf16)
            for m in range(MB):
                held[m, part] = image[:, m * lanes : (m + 1) * lanes].T

            @pl.when(has_target[direction])
            def _():
                send(direction, 0, part).start()

        @pl.when(has_target[direction])
        def _():
            for part in range(CHUNKS):
                send(direction, 1, part).start()

    for copy in small[2:]:
        copy.wait()
    row = lax.broadcasted_iota(jnp.int32, order.shape, 0)
    column = lax.broadcasted_iota(jnp.int32, order.shape, 1)
    order[...] = jnp.where(column == (row % 2) * lanes + row // 2, 1.0, 0.0).astype(bf16)

    @pl.when(i == 0)
    def _():
        west[...] = jnp.zeros_like(west)

    @pl.when(j == 0)
    def _():
        south[...] = jnp.zeros_like(south)

    for m in range(MB):
        site_col[m] = jnp.broadcast_to(site_row[m], (lanes, lanes)).T
        amp_col[m] = jnp.broadcast_to(amp_row[m], (lanes, lanes)).T
    for c in range(2):
        value = jnp.full(cells.shape, contrast[c, 0], f32)
        for k in range(1, contrast.shape[1]):
            value = jnp.where(cells[...] == k, contrast[c, k], value)
        fac[c] = value
    for c in range(2):
        for a in range(rows // lanes):
            block = pl.ds(a * lanes, lanes)
            ops_t[c, :, block] = ops[c, block, :].T

    def excite(m, buffer, slot, part, base):
        for a in range(piece // lanes):
            x = buffer[slot, part, :, pl.ds(a * lanes, lanes)].astype(f32)
            row = base // lanes + a
            fr, fi = fac[0, pl.ds(row, 1), :], fac[1, pl.ds(row, 1), :]
            points = lax.broadcasted_iota(jnp.int32, (lanes, lanes), 1) + row * lanes
            source = jnp.where(points == site_col[m], amp_col[m], 0.0)
            y_real = (fr * x[:nb] - fi * x[nb:] + source[:nb]).astype(bf16)
            y_imag = (fr * x[nb:] + fi * x[:nb] + source[nb:]).astype(bf16)
            block = pl.ds(base + a * lanes, lanes)
            excited[0, :nb, block] = y_real
            excited[0, nb:, block] = y_imag
            excited[1, :nb, block] = -y_imag
            excited[1, nb:, block] = y_real

    def product(depth, columns):
        return jnp.dot(
            excited[0, :, depth], ops_t[0, depth, columns], preferred_element_type=f32
        ) + jnp.dot(excited[1, :, depth], ops_t[1, depth, columns], preferred_element_type=f32)

    def gather(turn):
        m = turn % MB
        slot = turn - MB

        @pl.when(has_source[1])
        def _():
            for part in range(CHUNKS):
                send(1, slot, part).wait_recv()

        for part in range(CHUNKS):
            excite(m, west, slot, part, part * piece)
        total[...] = product(slice(0, face), slice(0, rows))
        for part in range(CHUNKS):
            @pl.when(has_source[0])
            def _():
                send(0, slot, part).wait_recv()

            start = face + part * piece
            excite(m, south, slot, part, start)
            if part < CHUNKS - 1:
                total[...] += product(slice(start, start + piece), slice(0, rows))

    last_piece = slice(rows - piece, rows)

    def turn_body(turn, _):
        gather(turn)
        for direction in range(2):
            held = (north_out, east_out)[direction]
            columns = slice(bases[direction], bases[direction] + face)
            image = (total[:, columns] + product(last_piece, columns)).astype(bf16)

            @pl.when(turn < SENDS)
            def _():
                for part in range(CHUNKS):
                    held[turn, part] = image[:, part * piece : (part + 1) * piece]

                @pl.when(has_target[direction])
                def _():
                    for part in range(CHUNKS):
                        send(direction, turn, part).start()

            @pl.when(turn == TURNS - 2)
            def _():
                final[0, nb:, columns] = image[:nb]
                final[1, nb:, columns] = image[nb:]

        return 0

    lax.fori_loop(MB, TURNS - 1, turn_body, 0)

    gather(TURNS - 1)
    for start in range(0, rows, 2 * lanes):
        columns = slice(start, start + 2 * lanes)
        image = (total[:, columns] + product(last_piece, columns)).astype(bf16)
        for a in range(2):
            part = slice(a * lanes, (a + 1) * lanes)
            block = slice(start + a * lanes, start + (a + 1) * lanes)
            real = jnp.concatenate([image[:nb, part], final[0, nb:, block]], axis=0)
            imag = jnp.concatenate([image[nb:, part], final[1, nb:, block]], axis=0)
            out_ref[pl.ds(2 * (start + a * lanes), 2 * lanes), :] = lax.dot_general(
                order[...],
                jnp.concatenate([real, imag], axis=1),
                (((1,), (1,)), ((), ())),
                preferred_element_type=f32,
            ).astype(bf16)

    for direction in (0, 1):
        @pl.when(has_target[direction])
        def _():
            for turn in range(SENDS):
                for part in range(CHUNKS):
                    send(direction, turn, part).wait_send()


def per_device(nx, ny, green_ops, cell_map, dipole_site, dipole_amp, contrast):
    rows = green_ops.shape[-1]
    lanes = dipole_site.shape[-1]
    face = rows // 2
    bf16, f32, i32 = jnp.bfloat16, jnp.float32, jnp.int32
    out = pl.pallas_call(
        functools.partial(kernel, nx, ny),
        out_shape=pltpu.VMEM((2 * rows, lanes), bf16),
        in_specs=[pl.BlockSpec(memory_space=pl.ANY)] * 5,
        out_specs=pl.BlockSpec(memory_space=pltpu.VMEM),
        scratch_shapes=[
            pltpu.VMEM((2, rows, rows), bf16),
            pltpu.VMEM((2, rows, rows), bf16),
            pltpu.VMEM((rows // lanes, lanes), i32),
            pltpu.VMEM((1, lanes), i32),
            pltpu.VMEM((2, lanes), f32),
            pltpu.SMEM(contrast.shape[::-1], f32),
            pltpu.VMEM((MB, lanes, lanes), i32),
            pltpu.VMEM((MB, lanes, lanes), f32),
            pltpu.VMEM((2, rows // lanes, lanes), f32),
            pltpu.VMEM((2, rows, MB * lanes), bf16),
            pltpu.VMEM((2, lanes, rows), bf16),
            pltpu.VMEM((lanes, rows), f32),
            *[pltpu.VMEM((SENDS, CHUNKS, lanes, face // CHUNKS), bf16)] * 4,
            pltpu.VMEM((2, lanes, rows), bf16),
            pltpu.VMEM((2 * lanes, 2 * lanes), bf16),
            pltpu.SemaphoreType.DMA((2, CHUNKS)),
            pltpu.SemaphoreType.DMA((4,)),
            pltpu.SemaphoreType.DMA((2, SENDS, CHUNKS)),
            pltpu.SemaphoreType.DMA((2, SENDS, CHUNKS)),
        ],
        compiler_params=pltpu.CompilerParams(collective_id=0, has_side_effects=True),
    )(
        green_ops[0, 0],
        cell_map.reshape(rows // lanes, lanes),
        dipole_site.reshape(1, lanes),
        dipole_amp[0, 0],
        contrast.T,
    )
    return out.reshape(1, 1, rows, 2, lanes)


def solution(mesh):
    placed = (
        P("gx", "gy", None, None, None),
        P("gx", "gy", None),
        P("gx", "gy", None),
        P("gx", "gy", None, None),
        P(),
    )
    return jax.shard_map(
        functools.partial(per_device, mesh.shape["gx"], mesh.shape["gy"]),
        mesh=mesh,
        in_specs=placed,
        out_specs=P("gx", "gy", None, None, None),
        check_vma=False,
    )
```

```python
import functools

import jax
import jax.numpy as jnp
from jax import lax
from jax.experimental import pallas as pl
from jax.experimental.pallas import tpu as pltpu
from jax.sharding import PartitionSpec as P

MB = 2
STEPS = 4
CHUNKS = 2
TURNS = MB * STEPS - 1
SENDS = TURNS - MB
MESH = pl.DeviceIdType.MESH


def kernel(
    nx, ny, ops_hbm, cells_hbm, site_hbm, amp_hbm, contrast_hbm, out_ref,
    ops, ops_t, cells, site, amp, contrast, site_col, amp_col, fac, first, excited, total,
    west, south, east_out, north_out, final, order, ops_sem, small_sem, send_sem, recv_sem,
):
    i = lax.axis_index("gx")
    j = lax.axis_index("gy")
    rows = ops.shape[1]
    face = rows // 2
    lanes = site.shape[1]
    nb = lanes // 2
    piece = face // CHUNKS
    bf16, f32 = jnp.bfloat16, jnp.float32
    bases = (face, 0)

    def ops_copy(direction, part):
        block = pl.ds(bases[direction] + part * piece, piece)
        return pltpu.make_async_copy(
            ops_hbm.at[:, block], ops.at[:, block], ops_sem.at[direction, part]
        )

    small = [
        pltpu.make_async_copy(src, dst, small_sem.at[k])
        for k, (src, dst) in enumerate(
            [(site_hbm, site), (amp_hbm, amp), (cells_hbm, cells), (contrast_hbm, contrast)]
        )
    ]
    for copy in small:
        copy.start()
    for direction in range(2):
        for part in range(CHUNKS):
            ops_copy(direction, part).start()

    barrier = pltpu.get_barrier_semaphore()

    @pl.when(i > 0)
    def _():
        pl.semaphore_signal(barrier, inc=1, device_id={"gx": i - 1}, device_id_type=MESH)

    @pl.when(j > 0)
    def _():
        pl.semaphore_signal(barrier, inc=1, device_id={"gy": j - 1}, device_id_type=MESH)

    for copy in small[:2]:
        copy.wait()

    low = lax.broadcasted_iota(jnp.int32, (1, lanes), 1) < nb
    sites = site[...]
    sites_turned = pltpu.roll(sites, nb, axis=1)
    real, imag = amp[0:1, :], amp[1:2, :]
    real_turned, imag_turned = pltpu.roll(real, nb, axis=1), pltpu.roll(imag, nb, axis=1)
    site_row = (jnp.where(low, sites, sites_turned), jnp.where(low, sites_turned, sites))
    amp_row = (jnp.where(low, real, imag_turned), jnp.where(low, real_turned, imag))
    turned_row = (jnp.where(low, -imag, real_turned), jnp.where(low, -imag_turned, real))
    for a in range(rows // lanes):
        block = pl.ds(a * lanes, lanes)
        points = lax.broadcasted_iota(jnp.int32, (lanes, lanes), 0) + a * lanes
        for m in range(MB):
            hit = points == site_row[m]
            columns = pl.ds(m * lanes, lanes)
            first[0, block, columns] = jnp.where(hit, amp_row[m], 0.0).astype(bf16)
            first[1, block, columns] = jnp.where(hit, turned_row[m], 0.0).astype(bf16)

    targets = jnp.where(i < nx - 1, 1, 0) + jnp.where(j < ny - 1, 1, 0)

    @pl.when(targets > 0)
    def _():
        pl.semaphore_wait(barrier, targets)

    def send(direction, turn, part):
        source, target, to = (
            (north_out, south, {"gy": j + 1}) if direction == 0 else (east_out, west, {"gx": i + 1})
        )
        return pltpu.make_async_remote_copy(
            src_ref=source.at[turn, part],
            dst_ref=target.at[turn, part],
            send_sem=send_sem.at[direction, turn, part],
            recv_sem=recv_sem.at[direction, turn, part],
            device_id=to,
            device_id_type=MESH,
        )

    has_target = (j < ny - 1, i < nx - 1)
    has_source = (j > 0, i > 0)

    for direction in range(2):
        held = (north_out, east_out)[direction]
        for part in range(CHUNKS):
            ops_copy(direction, part).wait()
            block = pl.ds(bases[direction] + part * piece, piece)
            image = jnp.dot(ops[0, block, :], first[0], preferred_element_type=f32) + jnp.dot(
                ops[1, block, :], first[1], preferred_element_type=f32
            )
            image = image.astype(bf16)
            for m in range(MB):
                held[m, part] = image[:, m * lanes : (m + 1) * lanes].T

            @pl.when(has_target[direction])
            def _():
                send(direction, 0, part).start()

        @pl.when(has_target[direction])
        def _():
            for part in range(CHUNKS):
                send(direction, 1, part).start()

    for copy in small[2:]:
        copy.wait()
    row = lax.broadcasted_iota(jnp.int32, order.shape, 0)
    column = lax.broadcasted_iota(jnp.int32, order.shape, 1)
    order[...] = jnp.where(column == (row % 2) * lanes + row // 2, 1.0, 0.0).astype(bf16)

    @pl.when(i == 0)
    def _():
        west[...] = jnp.zeros_like(west)

    @pl.when(j == 0)
    def _():
        south[...] = jnp.zeros_like(south)

    for m in range(MB):
        site_col[m] = jnp.broadcast_to(site_row[m], (lanes, lanes)).T
        amp_col[m] = jnp.broadcast_to(amp_row[m], (lanes, lanes)).T
    for c in range(2):
        value = jnp.full(cells.shape, contrast[c, 0], f32)
        for k in range(1, contrast.shape[1]):
            value = jnp.where(cells[...] == k, contrast[c, k], value)
        fac[c] = value
    for c in range(2):
        for a in range(rows // lanes):
            block = pl.ds(a * lanes, lanes)
            ops_t[c, :, block] = ops[c, block, :].T

    def excite(m, buffer, slot, part, base):
        for a in range(piece // lanes):
            x = buffer[slot, part, :, pl.ds(a * lanes, lanes)].astype(f32)
            row = base // lanes + a
            fr, fi = fac[0, pl.ds(row, 1), :], fac[1, pl.ds(row, 1), :]
            points = lax.broadcasted_iota(jnp.int32, (lanes, lanes), 1) + row * lanes
            source = jnp.where(points == site_col[m], amp_col[m], 0.0)
            y_real = (fr * x[:nb] - fi * x[nb:] + source[:nb]).astype(bf16)
            y_imag = (fr * x[nb:] + fi * x[:nb] + source[nb:]).astype(bf16)
            block = pl.ds(base + a * lanes, lanes)
            excited[0, :nb, block] = y_real
            excited[0, nb:, block] = y_imag
            excited[1, :nb, block] = -y_imag
            excited[1, nb:, block] = y_real

    def product(depth, columns):
        return jnp.dot(
            excited[0, :, depth], ops_t[0, depth, columns], preferred_element_type=f32
        ) + jnp.dot(excited[1, :, depth], ops_t[1, depth, columns], preferred_element_type=f32)

    def gather(turn):
        m = turn % MB
        slot = turn - MB

        @pl.when(has_source[1])
        def _():
            for part in range(CHUNKS):
                send(1, slot, part).wait_recv()

        for part in range(CHUNKS):
            excite(m, west, slot, part, part * piece)
        total[...] = product(slice(0, face), slice(0, rows))
        for part in range(CHUNKS):
            @pl.when(has_source[0])
            def _():
                send(0, slot, part).wait_recv()

            start = face + part * piece
            excite(m, south, slot, part, start)
            if part < CHUNKS - 1:
                total[...] += product(slice(start, start + piece), slice(0, rows))

    last_piece = slice(rows - piece, rows)

    def turn_body(turn, _):
        gather(turn)
        for direction in range(2):
            held = (north_out, east_out)[direction]
            columns = slice(bases[direction], bases[direction] + face)
            image = (total[:, columns] + product(last_piece, columns)).astype(bf16)

            @pl.when(turn < SENDS)
            def _():
                for part in range(CHUNKS):
                    held[turn, part] = image[:, part * piece : (part + 1) * piece]

                @pl.when(has_target[direction])
                def _():
                    for part in range(CHUNKS):
                        send(direction, turn, part).start()

            @pl.when(turn == TURNS - 2)
            def _():
                final[0, nb:, columns] = image[:nb]
                final[1, nb:, columns] = image[nb:]

        return 0

    lax.fori_loop(MB, TURNS - 1, turn_body, 0)

    gather(TURNS - 1)
    image = (total[...] + product(last_piece, slice(0, rows))).astype(bf16)
    for a in range(rows // lanes):
        block = slice(a * lanes, (a + 1) * lanes)
        real = jnp.concatenate([image[:nb, block], final[0, nb:, block]], axis=0)
        imag = jnp.concatenate([image[nb:, block], final[1, nb:, block]], axis=0)
        out_ref[pl.ds(2 * a * lanes, 2 * lanes), :] = lax.dot_general(
            order[...],
            jnp.concatenate([real, imag], axis=1),
            (((1,), (1,)), ((), ())),
            preferred_element_type=f32,
        ).astype(bf16)

    for direction in (0, 1):
        @pl.when(has_target[direction])
        def _():
            for turn in range(SENDS):
                for part in range(CHUNKS):
                    send(direction, turn, part).wait_send()


def per_device(nx, ny, green_ops, cell_map, dipole_site, dipole_amp, contrast):
    rows = green_ops.shape[-1]
    lanes = dipole_site.shape[-1]
    face = rows // 2
    bf16, f32, i32 = jnp.bfloat16, jnp.float32, jnp.int32
    out = pl.pallas_call(
        functools.partial(kernel, nx, ny),
        out_shape=pltpu.VMEM((2 * rows, lanes), bf16),
        in_specs=[pl.BlockSpec(memory_space=pl.ANY)] * 5,
        out_specs=pl.BlockSpec(memory_space=pltpu.VMEM),
        scratch_shapes=[
            pltpu.VMEM((2, rows, rows), bf16),
            pltpu.VMEM((2, rows, rows), bf16),
            pltpu.VMEM((rows // lanes, lanes), i32),
            pltpu.VMEM((1, lanes), i32),
            pltpu.VMEM((2, lanes), f32),
            pltpu.SMEM(contrast.shape[::-1], f32),
            pltpu.VMEM((MB, lanes, lanes), i32),
            pltpu.VMEM((MB, lanes, lanes), f32),
            pltpu.VMEM((2, rows // lanes, lanes), f32),
            pltpu.VMEM((2, rows, MB * lanes), bf16),
            pltpu.VMEM((2, lanes, rows), bf16),
            pltpu.VMEM((lanes, rows), f32),
            *[pltpu.VMEM((SENDS, CHUNKS, lanes, face // CHUNKS), bf16)] * 4,
            pltpu.VMEM((2, lanes, rows), bf16),
            pltpu.VMEM((2 * lanes, 2 * lanes), bf16),
            pltpu.SemaphoreType.DMA((2, CHUNKS)),
            pltpu.SemaphoreType.DMA((4,)),
            pltpu.SemaphoreType.DMA((2, SENDS, CHUNKS)),
            pltpu.SemaphoreType.DMA((2, SENDS, CHUNKS)),
        ],
        compiler_params=pltpu.CompilerParams(collective_id=0, has_side_effects=True),
    )(
        green_ops[0, 0],
        cell_map.reshape(rows // lanes, lanes),
        dipole_site.reshape(1, lanes),
        dipole_amp[0, 0],
        contrast.T,
    )
    return out.reshape(1, 1, rows, 2, lanes)


def solution(mesh):
    placed = (
        P("gx", "gy", None, None, None),
        P("gx", "gy", None),
        P("gx", "gy", None),
        P("gx", "gy", None, None),
        P(),
    )
    return jax.shard_map(
        functools.partial(per_device, mesh.shape["gx"], mesh.shape["gy"]),
        mesh=mesh,
        in_specs=placed,
        out_specs=P("gx", "gy", None, None, None),
        check_vma=False,
    )
```
